512 devices in a mesh: build: 128 (over z, y, core), prop: 4 (over x).
Axes of the slice: x: 4, y: 8, z: 8, core: 2. Of those that a mesh axis runs over, the one named last changes fastest.
Arguments:
- cholesky: bfloat16 [48, 2048, 2048], P(None, 'build'), may hold values from -0.09375 to 0.09375
- half_vectors: bfloat16 [48, 2048, 128], P(None, 'build'), may hold values from -0.00390625 to 0.00390625
- walkers: bfloat16 [512, 2048, 128], P(('build', 'prop')), may hold values from -6 to 6
- inverse_intersection: bfloat16 [512, 128, 128], P(('build', 'prop')), may hold values from -1.5 to 2.5
- fields: float32 [512, 48], replicated, may hold values from -6 to 6
- weights: float32 [512], replicated, may hold values from 0.5 to 2
- sources: int32 [512], replicated, may hold values from 0 to 511, as said below
Outputs:
- new_walkers: bfloat16 [512, 2048, 128], P(('build', 'prop'))
- new_weights: float32 [512], P(('build', 'prop'))
The draws below stay inside these ranges and needn't reach their ends.
Inputs may be any that keep to these rules, and one draw needn't show every extreme that they name: sources[w] has the same remainder modulo 4 as w; walkers 0 and 511 continue their own states.
All inputs are finite; a program needn't handle non-finite values.
Results may differ from the reference program's by a relative error of at most 0.014.
Values may be sent and summed in bfloat16 or wider, within the bound.
No kernel may reach another device: no remote copies, remote signals or barrier semaphores. Data moves between devices by JAX's collectives and lax.ppermute only.
A program may use at most 64 MiB of HBM per device.

```python
import math
import jax
import jax.numpy as jnp
from jax import lax

ORB = 2048
NEL = 128
CHOL = 48
ORDER = 6
GROUPS = 4
PER_GROUP = 128
WALKERS = 512


def draw_sources(key, part):
    walker = jnp.arange(WALKERS, dtype=jnp.int32)
    picked = jax.random.randint(key, (WALKERS,), 0, PER_GROUP, dtype=jnp.int32)
    picked = jnp.where(walker == 0, 0, picked)
    picked = jnp.where(walker == WALKERS - 1, PER_GROUP - 1, picked)
    return picked * GROUPS + walker % GROUPS


def draw_inverse_intersection(key, part):
    noise = jax.random.normal(key, (WALKERS, NEL, NEL), jnp.float32)
    values = jnp.eye(NEL, dtype=jnp.float32)[None] + 0.5 * noise * NEL ** (-0.5)
    return jnp.clip(values, -1.5, 2.5).astype(jnp.bfloat16)


def steps_of(rng, dims, cuts, least, top_value):
    factor_of = 1.0
    for position, shards_of in cuts:
        heights = jax.random.uniform(jax.random.fold_in(jax.random.fold_in(rng, 6), position), (shards_of,), jnp.float32, least / len(cuts), top_value / len(cuts))
        factor_of = factor_of * jnp.repeat(jnp.exp(heights), dims[position] // shards_of).reshape((-1,) + (1,) * (len(dims) - 1 - position))
    return factor_of


def bell_draw(rng, extent, deviation, limit, cuts=(), held_as=jnp.bfloat16):
    array = deviation * jax.random.normal(rng, extent, jnp.float32)
    if cuts:
        array = array * steps_of(rng, extent, cuts, -0.22, 0.18)
    return jnp.clip(array, -limit, limit).astype(held_as)


def setup_inputs(seed: int = 0) -> dict:
    splits = jax.random.split(jax.random.key(seed), 8)
    return {
        "cholesky": bell_draw(splits[0], (CHOL, ORB, ORB), (2.0 * (CHOL * ORB) ** -0.5), 0.09375, ((1, 128),)),
        "half_vectors": bell_draw(splits[1], (CHOL, ORB, NEL), (0.15 * (ORB * NEL) ** -0.5), 0.00390625, ((1, 128),)),
        "walkers": bell_draw(splits[2], (WALKERS, ORB, NEL), 1.0, 6.0, ((0, 512),)),
        "inverse_intersection": draw_inverse_intersection(jax.random.fold_in(splits[7], 71), 0),
        "fields": bell_draw(splits[4], (WALKERS, CHOL), 1.0, 6.0, (), jnp.float32),
        "weights": jnp.clip(jnp.exp(jax.random.uniform(splits[5], (WALKERS,), jnp.float32, math.log(0.5), math.log(2.0))), 0.5, 2.0),
        "sources": draw_sources(jax.random.fold_in(splits[7], 71), 0),
    }


def reference(cholesky, half_vectors, walkers, inverse_intersection, fields, weights, sources):
    walker_count = walkers.shape[0]
    half_wide = half_vectors.astype(jnp.float32)

    def bias_of(walker_pair):
        walker_state, inverse = walker_pair
        theta_full = jnp.dot(walker_state, inverse, preferred_element_type=jnp.float32).astype(jnp.bfloat16)
        return jnp.einsum("gqi,qi->g", half_wide, theta_full.astype(jnp.float32))

    force_bias = lax.map(bias_of, (walkers, inverse_intersection))
    exponent = jnp.sum(force_bias * (fields - 0.5 * force_bias), axis=-1)
    grown_weights = weights * jnp.exp(exponent)
    overall = jnp.sum(grown_weights)
    new_weights = jnp.take(grown_weights, sources, axis=0) * walker_count / overall
    coeffs = (fields - force_bias).astype(jnp.bfloat16)
    flat_vectors = cholesky.reshape(CHOL, ORB * ORB)

    def propagate(walker):
        source = lax.dynamic_index_in_dim(sources, walker, 0, False).astype(jnp.int32)
        coeff_row = lax.dynamic_slice_in_dim(coeffs, source, 1, 0)
        potential = jnp.dot(coeff_row, flat_vectors, preferred_element_type=jnp.float32)
        potential = potential.astype(jnp.bfloat16).reshape(ORB, ORB)
        begin_state = lax.dynamic_index_in_dim(walkers, source, 0, False)
        summed = begin_state.astype(jnp.float32)
        current = begin_state
        for degree in range(1, ORDER + 1):
            product = jnp.dot(potential, current, preferred_element_type=jnp.float32) / degree
            summed = summed + product
            current = product.astype(jnp.bfloat16)
        return summed.astype(jnp.bfloat16)

    new_walkers = lax.map(propagate, jnp.arange(walker_count, dtype=jnp.int32))
    return new_walkers, new_weights
```

```python
import functools

import jax
import jax.numpy as jnp
from jax import lax
from jax.experimental import pallas as pl
from jax.experimental.pallas import tpu as pltpu
from jax.sharding import Mesh
from jax.sharding import PartitionSpec as P

ORDER = 6
BUILD = ("build_0", "build_1", "build_2")
BUILD_PROP = ("build_0", "build_1", "build_2", "prop")


def spread(value, axis):
    count = lax.axis_size(axis)
    copies = jnp.broadcast_to(value[None], (count, *value.shape))
    return lax.all_to_all(copies, axis, split_axis=0, concat_axis=0, tiled=True)


def summed_over(value, axis):
    return jnp.sum(spread(value, axis), axis=0)


def tiles_kernel(rows, picks_ref, coeffs_ref, vectors_ref, out_ref):
    count, vectors = coeffs_ref.shape
    deep = vectors_ref.shape[0]
    high = picks_ref.shape[0]
    group = lax.broadcasted_iota(jnp.int32, (vectors, deep), 1) // rows
    widen = (group == lax.broadcasted_iota(jnp.int32, (vectors, deep), 0)).astype(jnp.bfloat16)
    wide = jnp.dot(coeffs_ref[...], widen, preferred_element_type=jnp.float32).astype(jnp.bfloat16)
    walker = lax.broadcasted_iota(jnp.int32, (high, count), 1)
    chosen = (walker == picks_ref[...]).astype(jnp.bfloat16)
    spread_out = jnp.dot(chosen, wide, preferred_element_type=jnp.float32)
    row = lax.broadcasted_iota(jnp.int32, (high, deep), 0) % rows
    column = lax.broadcasted_iota(jnp.int32, (high, deep), 1) % rows
    left = jnp.where(row == column, spread_out, 0.0).astype(jnp.bfloat16)
    out_ref[...] = jnp.dot(left, vectors_ref[...], preferred_element_type=jnp.float32).astype(
        out_ref.dtype
    )


def potential_tiles(picks, coeffs, cholesky):
    vectors, rows, orbitals = cholesky.shape
    count = coeffs.shape[0]
    flat = cholesky.reshape(vectors * rows, orbitals)
    block = 256
    tiles = pl.pallas_call(
        functools.partial(tiles_kernel, rows),
        grid=(count * rows // block,),
        in_specs=[
            pl.BlockSpec((block, 1), lambda i: (i, 0)),
            pl.BlockSpec((count, vectors), lambda i: (0, 0)),
            pl.BlockSpec((vectors * rows, orbitals), lambda i: (0, 0)),
        ],
        out_specs=pl.BlockSpec((block, orbitals), lambda i: (i, 0)),
        out_shape=jax.ShapeDtypeStruct((count * rows, orbitals), jnp.bfloat16),
        name="tiles",
    )(picks, coeffs, flat)
    return tiles.reshape(count, rows, orbitals)


def series_kernel(potential_ref, state_ref, out_ref, total_ref, term_ref):
    orbitals = potential_ref.shape[0]
    block = 256
    for degree in range(1, ORDER + 1):
        source = state_ref if degree == 1 else term_ref.at[(degree - 1) % 2]
        held = source[...]
        for at in range(0, orbitals, block):
            here = pl.ds(at, block)
            product = jnp.dot(potential_ref[here, :], held, preferred_element_type=jnp.float32)
            product = product / degree
            before = state_ref[here, :].astype(jnp.float32) if degree == 1 else total_ref[here, :]
            if degree == ORDER:
                out_ref[here, :] = (before + product).astype(out_ref.dtype)
            else:
                total_ref[here, :] = before + product
                term_ref[degree % 2, here, :] = product.astype(jnp.bfloat16)


def series(potential, state):
    orbitals, electrons = state.shape
    whole = pl.BlockSpec(memory_space=pltpu.VMEM)
    return pl.pallas_call(
        series_kernel,
        in_specs=[whole, whole],
        out_specs=whole,
        out_shape=jax.ShapeDtypeStruct((orbitals, electrons), jnp.bfloat16),
        scratch_shapes=[
            pltpu.VMEM((orbitals, electrons), jnp.float32),
            pltpu.VMEM((2, orbitals, electrons), jnp.bfloat16),
        ],
        name="series",
    )(potential, state)


def of_group(values, member, build_count, prop_count):
    split = values.reshape(build_count, prop_count, *values.shape[1:])
    return lax.dynamic_index_in_dim(split, member, 1, False)


def shards(cholesky, half_vectors, walkers, inverse_intersection, fields, weights, sources):
    build_count = lax.axis_size(BUILD)
    prop_count = lax.axis_size("prop")
    builder = lax.axis_index(BUILD)
    member = lax.axis_index("prop")
    orbitals = walkers.shape[1]
    electrons = walkers.shape[2]
    rows = orbitals // build_count
    own_state = walkers[0]
    theta = jnp.dot(
        own_state, inverse_intersection[0], preferred_element_type=jnp.float32
    ).astype(jnp.bfloat16)
    send = functools.partial(
        lax.all_to_all, axis_name=BUILD, split_axis=0, concat_axis=0, tiled=True
    )
    got_theta = send(theta.reshape(build_count, rows, electrons))
    got_state = send(own_state.reshape(build_count, rows, electrons))
    group_fields = of_group(fields, member, build_count, prop_count)
    group_weights = of_group(weights, member, build_count, prop_count)
    group_sources = of_group(sources, member, build_count, prop_count) // prop_count
    partial_bias = jnp.einsum(
        "wri,gri->wg", got_theta, half_vectors, preferred_element_type=jnp.float32
    )
    force_bias = summed_over(partial_bias, ("build_1", "build_2"))
    force_bias = summed_over(force_bias, "build_0")
    coeffs = (group_fields - force_bias).astype(jnp.bfloat16)
    picks = jnp.repeat(group_sources, rows)[:, None]
    tiles = potential_tiles(picks, coeffs, cholesky)
    starts = got_state.at[group_sources].get(mode="promise_in_bounds")
    begin_state = send(starts).reshape(orbitals, electrons)
    potential = send(tiles).reshape(orbitals, orbitals)
    exponent = jnp.sum(force_bias * (group_fields - 0.5 * force_bias), axis=-1)
    grown = group_weights * jnp.exp(exponent)
    overall = summed_over(jnp.sum(grown)[None], "prop")
    own_source = lax.dynamic_index_in_dim(group_sources, builder, 0, False)
    kept = lax.dynamic_index_in_dim(grown, own_source, 0, False)
    new_weight = kept * (build_count * prop_count) / overall
    stepped = series(potential, begin_state)
    return (stepped[None], new_weight.reshape(1))


def solution(mesh):
    torus = Mesh(
        mesh.devices.reshape(8, 8, 2, mesh.shape["prop"]), ("build_0", "build_1", "build_2", "prop")
    )
    return jax.shard_map(
        shards,
        mesh=torus,
        in_specs=(
            P(None, BUILD, None),
            P(None, BUILD, None),
            P(BUILD_PROP, None, None),
            P(BUILD_PROP, None, None),
            P(),
            P(),
            P(),
        ),
        out_specs=(P(BUILD_PROP, None, None), P(BUILD_PROP)),
        check_vma=False,
    )
```

```python
import functools

import jax
import jax.numpy as jnp
from jax import lax
from jax.experimental import pallas as pl
from jax.experimental.pallas import tpu as pltpu
from jax.sharding import Mesh
from jax.sharding import PartitionSpec as P

ORDER = 6
BUILD = ("build_0", "build_1", "build_2")
BUILD_PROP = ("build_0", "build_1", "build_2", "prop")


def spread(value, axis):
    count = lax.axis_size(axis)
    copies = jnp.broadcast_to(value[None], (count, *value.shape))
    return lax.all_to_all(copies, axis, split_axis=0, concat_axis=0, tiled=True)


def theta_kernel(state_ref, inverse_ref, out_ref):
    electrons = state_ref.shape[1]
    state = state_ref[...]
    out_ref[:, :electrons] = jnp.dot(
        state, inverse_ref[...], preferred_element_type=jnp.float32
    ).astype(out_ref.dtype)
    out_ref[:, electrons:] = state


def theta_and_state(state, inverse):
    orbitals, electrons = state.shape
    block = 512
    return pl.pallas_call(
        theta_kernel,
        grid=(orbitals // block,),
        in_specs=[
            pl.BlockSpec((block, electrons), lambda i: (i, 0)),
            pl.BlockSpec((electrons, electrons), lambda i: (0, 0)),
        ],
        out_specs=pl.BlockSpec((block, 2 * electrons), lambda i: (i, 0)),
        out_shape=jax.ShapeDtypeStruct((orbitals, 2 * electrons), state.dtype),
        name="theta",
    )(state, inverse)


def tiles_kernel(rows, chosen_ref, coeffs_ref, vectors_ref, out_ref, wide_ref):
    count, vectors = coeffs_ref.shape
    deep = vectors_ref.shape[0]
    block = out_ref.shape[0]
    few = block // rows
    shift = rows.bit_length() - 1
    step = pl.program_id(0)

    @pl.when(step == 0)
    def _():
        group = lax.broadcasted_iota(jnp.int32, (vectors, deep), 1) >> shift
        vector = lax.broadcasted_iota(jnp.int32, (vectors, deep), 0)
        widen = (group == vector).astype(jnp.bfloat16)
        picked = jnp.dot(chosen_ref[...], coeffs_ref[...], preferred_element_type=jnp.float32)
        wide_ref[...] = jnp.dot(
            picked.astype(jnp.bfloat16), widen, preferred_element_type=jnp.float32
        ).astype(jnp.bfloat16)

    owner = lax.broadcasted_iota(jnp.int32, (block, few), 0) >> shift
    repeat = (owner == lax.broadcasted_iota(jnp.int32, (block, few), 1)).astype(jnp.bfloat16)
    row = lax.broadcasted_iota(jnp.int32, (block, deep), 0) & (rows - 1)
    column = lax.broadcasted_iota(jnp.int32, (block, deep), 1) & (rows - 1)
    here = wide_ref[pl.ds(pl.multiple_of(step * few, few), few), :]
    left = jnp.dot(repeat, here, preferred_element_type=jnp.float32)
    left = jnp.where(row == column, left, 0.0).astype(jnp.bfloat16)
    out_ref[...] = jnp.dot(left, vectors_ref[...], preferred_element_type=jnp.float32).astype(
        out_ref.dtype
    )


def potential_tiles(chosen, coeffs, cholesky):
    vectors, rows, orbitals = cholesky.shape
    count = coeffs.shape[0]
    flat = cholesky.reshape(vectors * rows, orbitals)
    block = 256
    whole = pl.BlockSpec(memory_space=pltpu.VMEM)
    tiles = pl.pallas_call(
        functools.partial(tiles_kernel, rows),
        grid=(count * rows // block,),
        in_specs=[whole, whole, whole],
        out_specs=pl.BlockSpec((block, orbitals), lambda i: (i, 0)),
        out_shape=pltpu.HBM((count * rows, orbitals), jnp.bfloat16),
        scratch_shapes=[pltpu.VMEM((count, vectors * rows), jnp.bfloat16)],
        compiler_params=pltpu.CompilerParams(vmem_limit_bytes=16 << 20),
        name="tiles",
    )(chosen, coeffs, flat)
    return tiles.reshape(count, rows, orbitals)


def series_kernel(potential_ref, state_ref, out_ref, total_ref, term_ref):
    orbitals = potential_ref.shape[0]
    block = 256
    for degree in range(1, ORDER + 1):
        source = state_ref if degree == 1 else term_ref.at[(degree - 1) % 2]
        held = source[...]
        for at in range(0, orbitals, block):
            here = pl.ds(at, block)
            product = jnp.dot(potential_ref[here, :], held, preferred_element_type=jnp.float32)
            product = product / degree
            before = state_ref[here, :].astype(jnp.float32) if degree == 1 else total_ref[here, :]
            if degree == ORDER:
                out_ref[here, :] = (before + product).astype(out_ref.dtype)
            else:
                total_ref[here, :] = before + product
                term_ref[degree % 2, here, :] = product.astype(jnp.bfloat16)


def series(potential, state):
    orbitals, electrons = state.shape
    whole = pl.BlockSpec(memory_space=pltpu.VMEM)
    return pl.pallas_call(
        series_kernel,
        in_specs=[whole, whole],
        out_specs=whole,
        out_shape=jax.ShapeDtypeStruct((orbitals, electrons), jnp.bfloat16),
        scratch_shapes=[
            pltpu.VMEM((orbitals, electrons), jnp.float32),
            pltpu.VMEM((2, orbitals, electrons), jnp.bfloat16),
        ],
        compiler_params=pltpu.CompilerParams(vmem_limit_bytes=16 << 20),
        name="series",
    )(pltpu.with_memory_space_constraint(potential, pltpu.VMEM), state)


def of_group(values, member, build_count, prop_count):
    split = values.reshape(build_count, prop_count, *values.shape[1:])
    return lax.dynamic_index_in_dim(split, member, 1, False)


def shards(cholesky, half_vectors, walkers, inverse_intersection, fields, weights, sources):
    build_count = lax.axis_size(BUILD)
    prop_count = lax.axis_size("prop")
    builder = lax.axis_index(BUILD)
    member = lax.axis_index("prop")
    orbitals = walkers.shape[1]
    electrons = walkers.shape[2]
    rows = orbitals // build_count
    send = functools.partial(
        lax.all_to_all, axis_name=BUILD, split_axis=0, concat_axis=0, tiled=True
    )
    outgoing = theta_and_state(walkers[0], inverse_intersection[0])
    got = send(outgoing.reshape(build_count, rows, 2 * electrons))
    got_theta, got_state = got[:, :, :electrons], got[:, :, electrons:]
    group_fields = of_group(fields, member, build_count, prop_count)
    group_weights = of_group(weights, member, build_count, prop_count)
    group_sources = of_group(sources, member, build_count, prop_count) // prop_count
    partial_bias = jnp.einsum(
        "wri,gri->gw", got_theta, half_vectors, preferred_element_type=jnp.float32
    )
    starts = got_state.at[group_sources].get(mode="promise_in_bounds")
    starts, partial_bias = lax.optimization_barrier((starts, partial_bias))
    begin_state = send(starts).reshape(orbitals, electrons)
    line_bias = jnp.sum(lax.all_gather(partial_bias, ("build_1", "build_2")), axis=0)
    begin_state, line_bias = lax.optimization_barrier((begin_state, line_bias))
    force_bias = jnp.sum(spread(line_bias, "build_0"), axis=0).T
    coeffs = (group_fields - force_bias).astype(jnp.bfloat16)
    chosen = group_sources[:, None] == jnp.arange(build_count, dtype=jnp.int32)[None]
    tiles = potential_tiles(chosen.astype(jnp.bfloat16), coeffs, cholesky)
    exponent = jnp.sum(force_bias * (group_fields - 0.5 * force_bias), axis=-1)
    grown = group_weights * jnp.exp(exponent)
    overall = jnp.sum(spread(jnp.sum(grown)[None], "prop"), axis=0)
    own_source = lax.dynamic_index_in_dim(group_sources, builder, 0, False)
    kept = lax.dynamic_index_in_dim(grown, own_source, 0, False)
    new_weight = kept * (build_count * prop_count) / overall
    tiles, begin_state, new_weight = lax.optimization_barrier((tiles, begin_state, new_weight))
    potential = send(tiles).reshape(orbitals, orbitals)
    stepped = series(potential, begin_state)
    return (stepped[None], new_weight.reshape(1))


def solution(mesh):
    torus = Mesh(
        mesh.devices.reshape(8, 8, 2, mesh.shape["prop"]), ("build_0", "build_1", "build_2", "prop")
    )
    return jax.shard_map(
        shards,
        mesh=torus,
        in_specs=(
            P(None, BUILD, None),
            P(None, BUILD, None),
            P(BUILD_PROP, None, None),
            P(BUILD_PROP, None, None),
            P(),
            P(),
            P(),
        ),
        out_specs=(P(BUILD_PROP, None, None), P(BUILD_PROP)),
        check_vma=False,
    )
```

```python
import functools

import jax
import jax.numpy as jnp
from jax import lax
from jax.experimental import pallas as pl
from jax.experimental.pallas import tpu as pltpu
from jax.sharding import Mesh
from jax.sharding import PartitionSpec as P

ORDER = 6
BUILD = ("build_0", "build_1", "build_2")
BUILD_PROP = ("build_0", "build_1", "build_2", "prop")
WHOLE = pl.BlockSpec(memory_space=pltpu.VMEM)


def spread(value, axis):
    count = lax.axis_size(axis)
    copies = jnp.broadcast_to(value[None], (count, *value.shape))
    return lax.all_to_all(copies, axis, split_axis=0, concat_axis=0, tiled=True)


def theta_kernel(state_ref, inverse_ref, out_ref):
    electrons = state_ref.shape[1]
    state = state_ref[...]
    out_ref[:, :electrons] = jnp.dot(
        state, inverse_ref[...], preferred_element_type=jnp.float32
    ).astype(out_ref.dtype)
    out_ref[:, electrons:] = state


def theta_and_state(state, inverse):
    orbitals, electrons = state.shape
    return pl.pallas_call(
        theta_kernel,
        in_specs=[WHOLE, WHOLE],
        out_specs=WHOLE,
        out_shape=jax.ShapeDtypeStruct((orbitals, 2 * electrons), state.dtype),
        compiler_params=pltpu.CompilerParams(vmem_limit_bytes=8 << 20),
        name="theta",
    )(state, inverse)


def pick_kernel(prop_count, sources_ref, got_ref, theta_ref, starts_ref):
    count = got_ref.shape[0]
    electrons = theta_ref.shape[2]
    member = lax.axis_index("prop")
    theta_ref[...] = got_ref[:, :, :electrons]

    def move(w, carry):
        source = sources_ref[w * prop_count + member] // prop_count
        starts_ref[w] = got_ref[source, :, electrons:]
        return carry

    lax.fori_loop(0, count, move, 0, unroll=8)


def theta_and_starts(sources, got, prop_count):
    count, rows, both = got.shape
    shape = (count, rows, both // 2)
    return pl.pallas_call(
        functools.partial(pick_kernel, prop_count),
        in_specs=[pl.BlockSpec(memory_space=pltpu.SMEM), WHOLE],
        out_specs=[WHOLE, WHOLE],
        out_shape=[jax.ShapeDtypeStruct(shape, got.dtype), pltpu.HBM(shape, got.dtype)],
        compiler_params=pltpu.CompilerParams(vmem_limit_bytes=8 << 20),
        name="pick",
    )(sources, got)


def merge_kernel(parts_ref, out_ref):
    total = jnp.sum(parts_ref[...], axis=0)
    for at in range(out_ref.shape[0]):
        out_ref[at] = total


def summed_copies(parts, copies):
    return pl.pallas_call(
        merge_kernel,
        in_specs=[WHOLE],
        out_specs=WHOLE,
        out_shape=pltpu.HBM((copies, *parts.shape[1:]), parts.dtype),
        compiler_params=pltpu.CompilerParams(vmem_limit_bytes=8 << 20),
        name="merge",
    )(parts)


def bias_kernel(rows, parts_ref, fields_ref, weights_ref, sources_ref, own_ref, wide_ref, sums_ref, kept_ref):
    vectors, count = fields_ref.shape
    deep = wide_ref.shape[1]
    shift = rows.bit_length() - 1
    bias = jnp.sum(parts_ref[...], axis=0)
    fields = fields_ref[...]
    coeffs = (fields - bias).astype(jnp.bfloat16)
    exponent = jnp.sum(bias * (fields - 0.5 * bias), axis=0, keepdims=True)
    grown = weights_ref[...] * jnp.exp(exponent)
    kept = jnp.sum(grown * own_ref[...], axis=1, keepdims=True)
    kept_ref[...] = jnp.broadcast_to(kept, kept_ref.shape)
    total = jnp.sum(grown, axis=1, keepdims=True)
    sums_ref[...] = jnp.broadcast_to(total[None], sums_ref.shape)
    walker = lax.broadcasted_iota(jnp.int32, (count, count), 0)
    chosen = (walker == sources_ref[...]).astype(jnp.bfloat16)
    picked = jnp.dot(coeffs, chosen, preferred_element_type=jnp.float32).T
    group = lax.broadcasted_iota(jnp.int32, (vectors, deep), 1) >> shift
    vector = lax.broadcasted_iota(jnp.int32, (vectors, deep), 0)
    widen = (group == vector).astype(jnp.bfloat16)
    wide_ref[...] = jnp.dot(
        picked.astype(jnp.bfloat16), widen, preferred_element_type=jnp.float32
    ).astype(jnp.bfloat16)


def bias_and_weights(parts, fields, weights, sources, own, rows, prop_count):
    vectors, count = fields.shape
    return pl.pallas_call(
        functools.partial(bias_kernel, rows),
        in_specs=[WHOLE] * 5,
        out_specs=[WHOLE] * 3,
        out_shape=[
            pltpu.HBM((count, vectors * rows), jnp.bfloat16),
            pltpu.HBM((prop_count, 1, count), jnp.float32),
            jax.ShapeDtypeStruct((1, count), jnp.float32),
        ],
        compiler_params=pltpu.CompilerParams(vmem_limit_bytes=8 << 20),
        name="bias",
    )(parts, fields, weights, sources, own)


def tiles_kernel(rows, wide_ref, vectors_ref, out_ref):
    deep = vectors_ref.shape[0]
    block = out_ref.shape[0]
    few = block // rows
    shift = rows.bit_length() - 1
    step = pl.program_id(0)
    owner = lax.broadcasted_iota(jnp.int32, (block, few), 0) >> shift
    repeat = (owner == lax.broadcasted_iota(jnp.int32, (block, few), 1)).astype(jnp.bfloat16)
    row = lax.broadcasted_iota(jnp.int32, (block, deep), 0) & (rows - 1)
    column = lax.broadcasted_iota(jnp.int32, (block, deep), 1) & (rows - 1)
    here = wide_ref[pl.ds(pl.multiple_of(step * few, few), few), :]
    left = jnp.dot(repeat, here, preferred_element_type=jnp.float32)
    left = jnp.where(row == column, left, 0.0).astype(jnp.bfloat16)
    out_ref[...] = jnp.dot(left, vectors_ref[...], preferred_element_type=jnp.float32).astype(
        out_ref.dtype
    )


def potential_tiles(wide, cholesky):
    vectors, rows, orbitals = cholesky.shape
    count = wide.shape[0]
    flat = cholesky.reshape(vectors * rows, orbitals)
    block = 256
    tiles = pl.pallas_call(
        functools.partial(tiles_kernel, rows),
        grid=(count * rows // block,),
        in_specs=[WHOLE, WHOLE],
        out_specs=pl.BlockSpec((block, orbitals), lambda i: (i, 0)),
        out_shape=pltpu.HBM((count * rows, orbitals), jnp.bfloat16),
        compiler_params=pltpu.CompilerParams(vmem_limit_bytes=16 << 20),
        name="tiles",
    )(wide, flat)
    return tiles.reshape(count, rows, orbitals)


def series_kernel(potential_ref, state_ref, out_ref, total_ref, term_ref):
    orbitals = potential_ref.shape[0]
    block = 256
    for degree in range(1, ORDER + 1):
        source = state_ref if degree == 1 else term_ref.at[(degree - 1) % 2]
        held = source[...]
        for at in range(0, orbitals, block):
            here = pl.ds(at, block)
            product = jnp.dot(potential_ref[here, :], held, preferred_element_type=jnp.float32)
            product = product / degree
            before = state_ref[here, :].astype(jnp.float32) if degree == 1 else total_ref[here, :]
            if degree == ORDER:
                out_ref[here, :] = (before + product).astype(out_ref.dtype)
            else:
                total_ref[here, :] = before + product
                term_ref[degree % 2, here, :] = product.astype(jnp.bfloat16)


def series(potential, state):
    orbitals, electrons = state.shape
    return pl.pallas_call(
        series_kernel,
        in_specs=[WHOLE, WHOLE],
        out_specs=WHOLE,
        out_shape=jax.ShapeDtypeStruct((orbitals, electrons), jnp.bfloat16),
        scratch_shapes=[
            pltpu.VMEM((orbitals, electrons), jnp.float32),
            pltpu.VMEM((2, orbitals, electrons), jnp.bfloat16),
        ],
        compiler_params=pltpu.CompilerParams(vmem_limit_bytes=16 << 20),
        name="series",
    )(potential, state)


def of_group(values, member, build_count, prop_count):
    split = values.reshape(build_count, prop_count, *values.shape[1:])
    return lax.dynamic_index_in_dim(split, member, 1, False)


def shards(cholesky, half_vectors, walkers, inverse_intersection, fields, weights, sources):
    build_count = lax.axis_size(BUILD)
    prop_count = lax.axis_size("prop")
    builder = lax.axis_index(BUILD)
    member = lax.axis_index("prop")
    orbitals = walkers.shape[1]
    electrons = walkers.shape[2]
    rows = orbitals // build_count
    send = functools.partial(
        lax.all_to_all, axis_name=BUILD, split_axis=0, concat_axis=0, tiled=True
    )
    outgoing = theta_and_state(walkers[0], inverse_intersection[0])
    got = send(outgoing.reshape(build_count, rows, 2 * electrons))
    got_theta, starts = theta_and_starts(sources, got, prop_count)
    partial_bias = jnp.einsum(
        "wri,gri->gw", got_theta, half_vectors, preferred_element_type=jnp.float32
    )
    starts, partial_bias = lax.optimization_barrier((starts, partial_bias))
    begin_state = send(starts).reshape(orbitals, electrons)
    line_parts = lax.all_gather(partial_bias, ("build_1", "build_2"))
    begin_state, line_parts, fields, weights, sources = lax.optimization_barrier(
        (begin_state, line_parts, fields, weights, sources)
    )
    line_bias = summed_copies(line_parts, lax.axis_size("build_0"))
    parts = lax.all_to_all(line_bias, "build_0", split_axis=0, concat_axis=0, tiled=True)
    group_fields = of_group(fields, member, build_count, prop_count).T
    group_weights = of_group(weights, member, build_count, prop_count)[None]
    group_sources = of_group(sources, member, build_count, prop_count) // prop_count
    own_source = lax.dynamic_index_in_dim(group_sources, builder, 0, False)
    own = (jnp.arange(build_count, dtype=jnp.int32) == own_source).astype(jnp.float32)
    wide, sums, kept = bias_and_weights(
        parts, group_fields, group_weights, group_sources[None], own[None], rows, prop_count
    )
    sums = lax.all_to_all(sums, "prop", split_axis=0, concat_axis=0, tiled=True)
    tiles = potential_tiles(wide, cholesky)
    overall = jnp.sum(sums[:, 0, :1], axis=0)
    new_weight = kept[0, :1] * (build_count * prop_count) / overall
    tiles, begin_state, new_weight = lax.optimization_barrier((tiles, begin_state, new_weight))
    potential = send(tiles).reshape(orbitals, orbitals)
    potential = pltpu.with_memory_space_constraint(potential, pltpu.VMEM)
    stepped = series(potential, begin_state)
    return (stepped[None], new_weight)


def solution(mesh):
    torus = Mesh(
        mesh.devices.reshape(8, 8, 2, mesh.shape["prop"]), ("build_0", "build_1", "build_2", "prop")
    )
    return jax.shard_map(
        shards,
        mesh=torus,
        in_specs=(
            P(None, BUILD, None),
            P(None, BUILD, None),
            P(BUILD_PROP, None, None),
            P(BUILD_PROP, None, None),
            P(),
            P(),
            P(),
        ),
        out_specs=(P(BUILD_PROP, None, None), P(BUILD_PROP)),
        check_vma=False,
    )
```

```python
import functools

import jax
import jax.numpy as jnp
from jax import lax
from jax.experimental import pallas as pl
from jax.experimental.pallas import tpu as pltpu
from jax.sharding import Mesh
from jax.sharding import PartitionSpec as P

ORDER = 6
BUILD = ("build_0", "build_1", "build_2")
BUILD_PROP = ("build_0", "build_1", "build_2", "prop")
WHOLE = pl.BlockSpec(memory_space=pltpu.VMEM)


def in_hbm(value):
    return pltpu.with_memory_space_constraint(value, pltpu.HBM)


def whole_block(shape):
    return pl.BlockSpec(shape, lambda i: (0,) * len(shape))


def theta_kernel(state_ref, inverse_ref, out_ref):
    electrons = state_ref.shape[1]
    state = state_ref[...]
    out_ref[:, :electrons] = jnp.dot(
        state, inverse_ref[...], preferred_element_type=jnp.float32
    ).astype(out_ref.dtype)
    out_ref[:, electrons:] = state


def theta_and_state(state, inverse):
    orbitals, electrons = state.shape
    return pl.pallas_call(
        theta_kernel,
        grid=(1,),
        in_specs=[whole_block(state.shape), whole_block(inverse.shape)],
        out_specs=whole_block((orbitals, 2 * electrons)),
        out_shape=jax.ShapeDtypeStruct((orbitals, 2 * electrons), state.dtype),
        compiler_params=pltpu.CompilerParams(vmem_limit_bytes=8 << 20),
        name="theta",
    )(in_hbm(state), in_hbm(inverse))


def pick_kernel(prop_count, sources_ref, got_ref, theta_ref, starts_ref):
    count = got_ref.shape[0]
    electrons = theta_ref.shape[2]
    member = lax.axis_index("prop")
    theta_ref[...] = got_ref[:, :, :electrons]

    def move(w, carry):
        source = sources_ref[w * prop_count + member] // prop_count
        starts_ref[w] = got_ref[source, :, electrons:]
        return carry

    lax.fori_loop(0, count, move, 0, unroll=8)


def theta_and_starts(sources, got, prop_count):
    count, rows, both = got.shape
    shape = (count, rows, both // 2)
    return pl.pallas_call(
        functools.partial(pick_kernel, prop_count),
        in_specs=[pl.BlockSpec(memory_space=pltpu.SMEM), WHOLE],
        out_specs=[WHOLE, WHOLE],
        out_shape=[jax.ShapeDtypeStruct(shape, got.dtype), pltpu.HBM(shape, got.dtype)],
        compiler_params=pltpu.CompilerParams(vmem_limit_bytes=8 << 20),
        name="pick",
    )(in_hbm(sources), got)


def merge_kernel(parts_ref, out_ref):
    total = jnp.sum(parts_ref[...], axis=0)
    for at in range(out_ref.shape[0]):
        out_ref[at] = total


def summed_copies(parts, copies):
    return pl.pallas_call(
        merge_kernel,
        grid=(1,),
        in_specs=[whole_block(parts.shape)],
        out_specs=whole_block((copies, *parts.shape[1:])),
        out_shape=pltpu.HBM((copies, *parts.shape[1:]), parts.dtype),
        compiler_params=pltpu.CompilerParams(vmem_limit_bytes=8 << 20),
        name="merge",
    )(in_hbm(parts))


def bias_kernel(rows, parts_ref, fields_ref, weights_ref, sources_ref, wide_ref, sums_ref, kept_ref):
    vectors, walkers = fields_ref.shape
    count = parts_ref.shape[2]
    deep = wide_ref.shape[1]
    shift = rows.bit_length() - 1
    stride = walkers // count
    member = lax.axis_index("prop")
    builder = lax.axis_index(BUILD[0])
    for axis in BUILD[1:]:
        builder = builder * lax.axis_size(axis) + lax.axis_index(axis)
    exact = functools.partial(
        jnp.dot, precision=lax.Precision.HIGHEST, preferred_element_type=jnp.float32
    )
    place = lax.broadcasted_iota(jnp.int32, (walkers, count), 0)
    walker = lax.broadcasted_iota(jnp.int32, (walkers, count), 1)
    select = (place == walker * stride + member).astype(jnp.float32)
    fields = exact(fields_ref[...], select)
    weights = exact(weights_ref[...], select)
    sources = exact((sources_ref[...] // stride).astype(jnp.float32), select)
    bias = jnp.sum(parts_ref[...], axis=0)
    coeffs = (fields - bias).astype(jnp.bfloat16)
    exponent = jnp.sum(bias * (fields - 0.5 * bias), axis=0, keepdims=True)
    grown = weights * jnp.exp(exponent)
    lane = lax.broadcasted_iota(jnp.int32, (1, count), 1)
    own = jnp.sum(jnp.where(lane == builder, sources, 0.0), axis=1, keepdims=True)
    kept = jnp.where(lane.astype(jnp.float32) == own, grown, 0.0)
    kept_ref[...] = jnp.broadcast_to(jnp.sum(kept, axis=1, keepdims=True), kept_ref.shape)
    total = jnp.sum(grown, axis=1, keepdims=True)
    sums_ref[...] = jnp.broadcast_to(total[None], sums_ref.shape)
    row = lax.broadcasted_iota(jnp.int32, (count, count), 0).astype(jnp.float32)
    chosen = (row == sources).astype(jnp.bfloat16)
    picked = jnp.dot(coeffs, chosen, preferred_element_type=jnp.float32).T
    group = lax.broadcasted_iota(jnp.int32, (vectors, deep), 1) >> shift
    vector = lax.broadcasted_iota(jnp.int32, (vectors, deep), 0)
    widen = (group == vector).astype(jnp.bfloat16)
    wide_ref[...] = jnp.dot(
        picked.astype(jnp.bfloat16), widen, preferred_element_type=jnp.float32
    ).astype(jnp.bfloat16)


def bias_and_weights(parts, fields, weights, sources, rows, prop_count):
    vectors = fields.shape[0]
    count = parts.shape[2]
    arrays = (parts, fields, weights, sources)
    return pl.pallas_call(
        functools.partial(bias_kernel, rows),
        grid=(1,),
        in_specs=[whole_block(array.shape) for array in arrays],
        out_specs=[
            whole_block((count, vectors * rows)),
            whole_block((prop_count, 1, count)),
            whole_block((1, count)),
        ],
        out_shape=[
            jax.ShapeDtypeStruct((count, vectors * rows), jnp.bfloat16),
            jax.ShapeDtypeStruct((prop_count, 1, count), jnp.float32),
            jax.ShapeDtypeStruct((1, count), jnp.float32),
        ],
        compiler_params=pltpu.CompilerParams(vmem_limit_bytes=8 << 20),
        name="bias",
    )(*arrays)


def tiles_kernel(rows, wide_ref, vectors_ref, out_ref):
    deep = vectors_ref.shape[0]
    block = out_ref.shape[0]
    few = block // rows
    shift = rows.bit_length() - 1
    owner = lax.broadcasted_iota(jnp.int32, (block, few), 0) >> shift
    repeat = (owner == lax.broadcasted_iota(jnp.int32, (block, few), 1)).astype(jnp.bfloat16)
    row = lax.broadcasted_iota(jnp.int32, (block, deep), 0) & (rows - 1)
    column = lax.broadcasted_iota(jnp.int32, (block, deep), 1) & (rows - 1)
    left = jnp.dot(repeat, wide_ref[...], preferred_element_type=jnp.float32)
    left = jnp.where(row == column, left, 0.0).astype(jnp.bfloat16)
    out_ref[...] = jnp.dot(left, vectors_ref[...], preferred_element_type=jnp.float32).astype(
        out_ref.dtype
    )


def potential_tiles(wide, cholesky):
    vectors, rows, orbitals = cholesky.shape
    count = wide.shape[0]
    flat = cholesky.reshape(vectors * rows, orbitals)
    block = 512
    tiles = pl.pallas_call(
        functools.partial(tiles_kernel, rows),
        grid=(count * rows // block,),
        in_specs=[pl.BlockSpec((block // rows, vectors * rows), lambda i: (i, 0)), WHOLE],
        out_specs=pl.BlockSpec((block, orbitals), lambda i: (i, 0)),
        out_shape=pltpu.HBM((count * rows, orbitals), jnp.bfloat16),
        compiler_params=pltpu.CompilerParams(vmem_limit_bytes=20 << 20),
        name="tiles",
    )(wide, flat)
    return tiles.reshape(count, rows, orbitals)


def series_kernel(potential_ref, state_ref, out_ref, total_ref, term_ref):
    orbitals = potential_ref.shape[0]
    block = 256
    for degree in range(1, ORDER + 1):
        source = state_ref if degree == 1 else term_ref.at[(degree - 1) % 2]
        held = source[...]
        for at in range(0, orbitals, block):
            here = pl.ds(at, block)
            product = jnp.dot(potential_ref[here, :], held, preferred_element_type=jnp.float32)
            product = product / degree
            before = state_ref[here, :].astype(jnp.float32) if degree == 1 else total_ref[here, :]
            if degree == ORDER:
                out_ref[here, :] = (before + product).astype(out_ref.dtype)
            else:
                total_ref[here, :] = before + product
                term_ref[degree % 2, here, :] = product.astype(jnp.bfloat16)


def series(potential, state):
    orbitals, electrons = state.shape
    return pl.pallas_call(
        series_kernel,
        in_specs=[WHOLE, WHOLE],
        out_specs=WHOLE,
        out_shape=jax.ShapeDtypeStruct((orbitals, electrons), jnp.bfloat16),
        scratch_shapes=[
            pltpu.VMEM((orbitals, electrons), jnp.float32),
            pltpu.VMEM((2, orbitals, electrons), jnp.bfloat16),
        ],
        compiler_params=pltpu.CompilerParams(vmem_limit_bytes=16 << 20),
        name="series",
    )(potential, state)


def shards(cholesky, half_vectors, walkers, inverse_intersection, fields, weights, sources):
    build_count = lax.axis_size(BUILD)
    prop_count = lax.axis_size("prop")
    orbitals = walkers.shape[1]
    electrons = walkers.shape[2]
    rows = orbitals // build_count
    send = functools.partial(
        lax.all_to_all, axis_name=BUILD, split_axis=0, concat_axis=0, tiled=True
    )
    outgoing = theta_and_state(walkers[0], inverse_intersection[0])
    got = send(outgoing.reshape(build_count, rows, 2 * electrons))
    got_theta, starts = theta_and_starts(sources, got, prop_count)
    partial_bias = jnp.einsum(
        "wri,gri->gw", got_theta, half_vectors, preferred_element_type=jnp.float32
    )
    starts, partial_bias = lax.optimization_barrier((starts, partial_bias))
    begin_state = send(starts).reshape(orbitals, electrons)
    line_parts = lax.all_gather(partial_bias, ("build_1", "build_2"))
    begin_state, line_parts = lax.optimization_barrier((begin_state, line_parts))
    line_bias = summed_copies(line_parts, lax.axis_size("build_0"))
    parts = lax.all_to_all(line_bias, "build_0", split_axis=0, concat_axis=0, tiled=True)
    wide, sums, kept = bias_and_weights(
        parts, in_hbm(fields.T), in_hbm(weights[None]), in_hbm(sources[None]), rows, prop_count
    )
    sums = lax.all_to_all(sums, "prop", split_axis=0, concat_axis=0, tiled=True)
    tiles = potential_tiles(wide, cholesky)
    overall = jnp.sum(sums[:, 0, :1], axis=0)
    new_weight = kept[0, :1] * (build_count * prop_count) / overall
    tiles, begin_state, new_weight = lax.optimization_barrier((tiles, begin_state, new_weight))
    potential = send(tiles).reshape(orbitals, orbitals)
    potential = pltpu.with_memory_space_constraint(potential, pltpu.VMEM)
    stepped = series(potential, begin_state)
    return (stepped[None], new_weight)


def solution(mesh):
    torus = Mesh(
        mesh.devices.reshape(8, 8, 2, mesh.shape["prop"]), ("build_0", "build_1", "build_2", "prop")
    )
    return jax.shard_map(
        shards,
        mesh=torus,
        in_specs=(
            P(None, BUILD, None),
            P(None, BUILD, None),
            P(BUILD_PROP, None, None),
            P(BUILD_PROP, None, None),
            P(),
            P(),
            P(),
        ),
        out_specs=(P(BUILD_PROP, None, None), P(BUILD_PROP)),
        check_vma=False,
    )
```

```python
import functools

import jax
import jax.numpy as jnp
from jax import lax
from jax.experimental import pallas as pl
from jax.experimental.pallas import tpu as pltpu
from jax.sharding import Mesh
from jax.sharding import PartitionSpec as P

ORDER = 6
BUILD = ("build_0", "build_1", "build_2")
BUILD_PROP = ("build_0", "build_1", "build_2", "prop")
WHOLE = pl.BlockSpec(memory_space=pltpu.VMEM)


def in_hbm(value):
    return pltpu.with_memory_space_constraint(value, pltpu.HBM)


def whole_block(shape):
    return pl.BlockSpec(shape, lambda i: (0,) * len(shape))


def theta_kernel(state_ref, inverse_ref, out_ref):
    electrons = state_ref.shape[1]
    state = state_ref[...]
    out_ref[:, :electrons] = jnp.dot(
        state, inverse_ref[...], preferred_element_type=jnp.float32
    ).astype(out_ref.dtype)
    out_ref[:, electrons:] = state


def theta_and_state(state, inverse):
    orbitals, electrons = state.shape
    return pl.pallas_call(
        theta_kernel,
        grid=(1,),
        in_specs=[whole_block(state.shape), whole_block(inverse.shape)],
        out_specs=whole_block((orbitals, 2 * electrons)),
        out_shape=jax.ShapeDtypeStruct((orbitals, 2 * electrons), state.dtype),
        compiler_params=pltpu.CompilerParams(vmem_limit_bytes=8 << 20),
        name="theta",
    )(in_hbm(state), in_hbm(inverse))


def pick_kernel(prop_count, sources_ref, got_ref, theta_ref, starts_ref):
    count = got_ref.shape[0]
    electrons = theta_ref.shape[2]
    member = lax.axis_index("prop")
    theta_ref[...] = got_ref[:, :, :electrons]

    def move(w, carry):
        source = sources_ref[w * prop_count + member] // prop_count
        starts_ref[w] = got_ref[source, :, electrons:]
        return carry

    lax.fori_loop(0, count, move, 0, unroll=8)


def theta_and_starts(sources, got, prop_count):
    count, rows, both = got.shape
    shape = (count, rows, both // 2)
    return pl.pallas_call(
        functools.partial(pick_kernel, prop_count),
        in_specs=[pl.BlockSpec(memory_space=pltpu.SMEM), WHOLE],
        out_specs=[WHOLE, WHOLE],
        out_shape=[jax.ShapeDtypeStruct(shape, got.dtype), pltpu.HBM(shape, got.dtype)],
        compiler_params=pltpu.CompilerParams(vmem_limit_bytes=8 << 20),
        name="pick",
    )(in_hbm(sources), got)


def merge_kernel(parts_ref, out_ref):
    total = jnp.sum(parts_ref[...], axis=0)
    for at in range(out_ref.shape[0]):
        out_ref[at] = total


def summed_copies(parts, copies):
    return pl.pallas_call(
        merge_kernel,
        grid=(1,),
        in_specs=[whole_block(parts.shape)],
        out_specs=whole_block((copies, *parts.shape[1:])),
        out_shape=pltpu.HBM((copies, *parts.shape[1:]), parts.dtype),
        compiler_params=pltpu.CompilerParams(vmem_limit_bytes=8 << 20),
        name="merge",
    )(in_hbm(parts))


def bias_kernel(rows, parts_ref, fields_ref, weights_ref, sources_ref, wide_ref, sums_ref, kept_ref):
    vectors, walkers = fields_ref.shape
    count = parts_ref.shape[2]
    deep = wide_ref.shape[1]
    shift = rows.bit_length() - 1
    stride = walkers // count
    member = lax.axis_index("prop")
    builder = lax.axis_index(BUILD[0])
    for axis in BUILD[1:]:
        builder = builder * lax.axis_size(axis) + lax.axis_index(axis)
    exact = functools.partial(
        jnp.dot, precision=lax.Precision.HIGHEST, preferred_element_type=jnp.float32
    )
    place = lax.broadcasted_iota(jnp.int32, (walkers, count), 0)
    walker = lax.broadcasted_iota(jnp.int32, (walkers, count), 1)
    select = (place == walker * stride + member).astype(jnp.float32)
    fields = exact(fields_ref[...], select)
    weights = exact(weights_ref[...], select)
    sources = exact((sources_ref[...] // stride).astype(jnp.float32), select)
    bias = jnp.sum(parts_ref[...], axis=0)
    coeffs = (fields - bias).astype(jnp.bfloat16)
    exponent = jnp.sum(bias * (fields - 0.5 * bias), axis=0, keepdims=True)
    grown = weights * jnp.exp(exponent)
    lane = lax.broadcasted_iota(jnp.int32, (1, count), 1)
    own = jnp.sum(jnp.where(lane == builder, sources, 0.0), axis=1, keepdims=True)
    kept = jnp.where(lane.astype(jnp.float32) == own, grown, 0.0)
    kept_ref[...] = jnp.broadcast_to(jnp.sum(kept, axis=1, keepdims=True), kept_ref.shape)
    total = jnp.sum(grown, axis=1, keepdims=True)
    sums_ref[...] = jnp.broadcast_to(total[None], sums_ref.shape)
    row = lax.broadcasted_iota(jnp.int32, (count, count), 0).astype(jnp.float32)
    chosen = (row == sources).astype(jnp.bfloat16)
    picked = jnp.dot(coeffs, chosen, preferred_element_type=jnp.float32).T
    group = lax.broadcasted_iota(jnp.int32, (vectors, deep), 1) >> shift
    vector = lax.broadcasted_iota(jnp.int32, (vectors, deep), 0)
    widen = (group == vector).astype(jnp.bfloat16)
    wide_ref[...] = jnp.dot(
        picked.astype(jnp.bfloat16), widen, preferred_element_type=jnp.float32
    ).astype(jnp.bfloat16)


def bias_and_weights(parts, fields, weights, sources, rows, prop_count):
    vectors = fields.shape[0]
    count = parts.shape[2]
    arrays = (parts, fields, weights, sources)
    return pl.pallas_call(
        functools.partial(bias_kernel, rows),
        grid=(1,),
        in_specs=[whole_block(array.shape) for array in arrays],
        out_specs=[
            whole_block((count, vectors * rows)),
            whole_block((prop_count, 1, count)),
            whole_block((1, count)),
        ],
        out_shape=[
            jax.ShapeDtypeStruct((count, vectors * rows), jnp.bfloat16),
            jax.ShapeDtypeStruct((prop_count, 1, count), jnp.float32),
            jax.ShapeDtypeStruct((1, count), jnp.float32),
        ],
        compiler_params=pltpu.CompilerParams(vmem_limit_bytes=8 << 20),
        name="bias",
    )(*arrays)


def tiles_kernel(rows, wide_ref, vectors_ref, out_ref):
    deep = vectors_ref.shape[0]
    block = out_ref.shape[0]
    few = block // rows
    shift = rows.bit_length() - 1
    owner = lax.broadcasted_iota(jnp.int32, (block, few), 0) >> shift
    repeat = (owner == lax.broadcasted_iota(jnp.int32, (block, few), 1)).astype(jnp.bfloat16)
    row = lax.broadcasted_iota(jnp.int32, (block, deep), 0) & (rows - 1)
    column = lax.broadcasted_iota(jnp.int32, (block, deep), 1) & (rows - 1)
    left = jnp.dot(repeat, wide_ref[...], preferred_element_type=jnp.float32)
    left = jnp.where(row == column, left, 0.0).astype(jnp.bfloat16)
    out_ref[...] = jnp.dot(left, vectors_ref[...], preferred_element_type=jnp.float32).astype(
        out_ref.dtype
    )


def potential_tiles(wide, cholesky):
    vectors, rows, orbitals = cholesky.shape
    count = wide.shape[0]
    flat = cholesky.reshape(vectors * rows, orbitals)
    block = 512
    tiles = pl.pallas_call(
        functools.partial(tiles_kernel, rows),
        grid=(count * rows // block,),
        in_specs=[pl.BlockSpec((block // rows, vectors * rows), lambda i: (i, 0)), WHOLE],
        out_specs=pl.BlockSpec((block, orbitals), lambda i: (i, 0)),
        out_shape=pltpu.HBM((count * rows, orbitals), jnp.bfloat16),
        compiler_params=pltpu.CompilerParams(vmem_limit_bytes=20 << 20),
        name="tiles",
    )(wide, flat)
    return tiles.reshape(count, rows, orbitals)


def series_kernel(
    scale, potential_ref, state_ref, sums_ref, kept_ref, out_ref, weight_ref, total_ref, term_ref
):
    overall = jnp.sum(sums_ref[...], axis=0)
    weight = kept_ref[...] * scale / overall
    weight_ref[...] = weight[0, :1]
    orbitals = potential_ref.shape[0]
    block = 512
    for degree in range(1, ORDER + 1):
        source = state_ref if degree == 1 else term_ref.at[(degree - 1) % 2]
        held = source[...]
        for at in range(0, orbitals, block):
            here = pl.ds(at, block)
            product = jnp.dot(potential_ref[here, :], held, preferred_element_type=jnp.float32)
            product = product / degree
            before = state_ref[here, :].astype(jnp.float32) if degree == 1 else total_ref[here, :]
            if degree == ORDER:
                out_ref[here, :] = (before + product).astype(out_ref.dtype)
            else:
                total_ref[here, :] = before + product
                term_ref[degree % 2, here, :] = product.astype(jnp.bfloat16)


def series(potential, state, sums, kept, scale):
    orbitals, electrons = state.shape
    return pl.pallas_call(
        functools.partial(series_kernel, scale),
        in_specs=[WHOLE] * 4,
        out_specs=[WHOLE] * 2,
        out_shape=[
            jax.ShapeDtypeStruct((orbitals, electrons), jnp.bfloat16),
            jax.ShapeDtypeStruct((1,), jnp.float32),
        ],
        scratch_shapes=[
            pltpu.VMEM((orbitals, electrons), jnp.float32),
            pltpu.VMEM((2, orbitals, electrons), jnp.bfloat16),
        ],
        compiler_params=pltpu.CompilerParams(vmem_limit_bytes=16 << 20),
        name="series",
    )(potential, in_hbm(state), in_hbm(sums), in_hbm(kept))


def shards(cholesky, half_vectors, walkers, inverse_intersection, fields, weights, sources):
    build_count = lax.axis_size(BUILD)
    prop_count = lax.axis_size("prop")
    orbitals = walkers.shape[1]
    electrons = walkers.shape[2]
    rows = orbitals // build_count
    send = functools.partial(
        lax.all_to_all, axis_name=BUILD, split_axis=0, concat_axis=0, tiled=True
    )
    outgoing = theta_and_state(walkers[0], inverse_intersection[0])
    got = send(outgoing.reshape(build_count, rows, 2 * electrons))
    got_theta, starts = theta_and_starts(sources, got, prop_count)
    partial_bias = jnp.einsum(
        "wri,gri->gw", got_theta, half_vectors, preferred_element_type=jnp.float32
    )
    exchange = functools.partial(lax.all_to_all, split_axis=0, concat_axis=0, tiled=True)
    chip_parts = lax.all_gather(partial_bias, "build_2")
    chip_bias = summed_copies(chip_parts, lax.axis_size("build_1"))
    line_bias = summed_copies(exchange(chip_bias, "build_1"), lax.axis_size("build_0"))
    parts = exchange(line_bias, "build_0")
    starts, parts = lax.optimization_barrier((starts, parts))
    begin_state = send(starts).reshape(orbitals, electrons)
    wide, sums, kept = bias_and_weights(
        parts, in_hbm(fields.T), in_hbm(weights[None]), in_hbm(sources[None]), rows, 1
    )
    sums = lax.all_gather(sums[0], "prop")
    tiles = potential_tiles(wide, cholesky)
    tiles, begin_state, sums, kept = lax.optimization_barrier((tiles, begin_state, sums, kept))
    potential = send(tiles).reshape(orbitals, orbitals)
    potential = pltpu.with_memory_space_constraint(potential, pltpu.VMEM)
    scale = float(build_count * prop_count)
    stepped, new_weight = series(potential, begin_state, sums, kept, scale)
    return (stepped[None], new_weight)


def solution(mesh):
    torus = Mesh(
        mesh.devices.reshape(8, 8, 2, mesh.shape["prop"]), ("build_0", "build_1", "build_2", "prop")
    )
    return jax.shard_map(
        shards,
        mesh=torus,
        in_specs=(
            P(None, BUILD, None),
            P(None, BUILD, None),
            P(BUILD_PROP, None, None),
            P(BUILD_PROP, None, None),
            P(),
            P(),
            P(),
        ),
        out_specs=(P(BUILD_PROP, None, None), P(BUILD_PROP)),
        check_vma=False,
    )
```
